256 devices in a mesh: row: 32 (over y_lo, z, core), col: 8 (over x, y_hi).
Axes of the slice: x: 4, y: 4 (y_hi: 2, y_lo: 2; y = y_hi * 2 + y_lo), z: 8, core: 2. Of those that a mesh axis runs over, the one named last changes fastest.
Arguments:
- inverse_tiles: bfloat16 [128, 256, 128, 256], P('col', None, 'row'), may hold values from -6 to 6
- factor_panels: bfloat16 [2, 128, 256, 256], P(None, 'row', 'col'), may hold values from -0.0390625 to 0.0390625
- ancestors: int32 [2, 96], replicated, may hold values from 0 to 127, as said below
- valid_flags: int32 [2, 96], replicated, may hold values from 0 to 1, as said below
- block_slot: int32 [128], replicated, may hold values from 0 to 127, each once
Outputs:
- new_panels: float32 [128, 256, 2, 256], P('col', 'row')
The draws below stay inside these ranges and needn't reach their ends.
Inputs may be any that keep to these rules, and one draw needn't show every extreme that they name: `ancestors`: within one supernode's list all 96 entries name different blocks. `valid_flags`: each list's used entries come first; supernode 0's list is used in full, the others in 64 entries or more.
All inputs are finite; a program needn't handle non-finite values.
Results may differ from the reference program's by a relative error of at most 0.0003.
Values may be sent and summed in bfloat16 or wider, within the bound.
No kernel may reach another device: no remote copies, remote signals or barrier semaphores. Data moves between devices by JAX's collectives and lax.ppermute only.
A program may use at most 64 MiB of HBM per device.

```python
import jax
import jax.numpy as jnp
from jax import lax

BW = 256
NA = 96
NB = 128
SN = 2
N_ROW = 32


def lists_helper(key):
    base = jax.random.fold_in(key, 11)
    keys = jax.random.split(base, SN)
    block_ids = jax.vmap(lambda single: jax.random.permutation(single, NB)[:NA])(keys).astype(jnp.int32)
    counts = jax.random.randint(jax.random.fold_in(base, 5), (SN,), 2 * NA // 3, NA + 1).astype(jnp.int32)
    counts = counts.at[0].set(NA)
    flags = (jnp.arange(NA, dtype=jnp.int32)[None, :] < counts[:, None]).astype(jnp.int32)
    return (block_ids, flags)


def draw_ancestors(key, part):
    return lists_helper(key)[0]


def draw_valid_flags(key, part):
    return lists_helper(key)[1]


def steps_of(rng, extent, cuts, smallest, top_value):
    factor_of = 1.0
    for dim, blocks in cuts:
        draws = jax.random.uniform(jax.random.fold_in(jax.random.fold_in(rng, 6), dim), (blocks,), jnp.float32, smallest / len(cuts), top_value / len(cuts))
        factor_of = factor_of * jnp.repeat(jnp.exp(draws), extent[dim] // blocks).reshape((-1,) + (1,) * (len(extent) - 1 - dim))
    return factor_of


def noise(stream_key, extent, scale, most, shards=(), held_as=jnp.bfloat16):
    level = steps_of(stream_key, extent, shards, -0.22, 0.18) if shards else 1.0
    entries = jax.random.normal(stream_key, extent, jnp.float32) * scale * level
    return jnp.minimum(jnp.maximum(entries, -most), most).astype(held_as)


def setup_inputs(seed: int = 0) -> dict:
    seeds = jax.random.split(jax.random.key(seed), 6)
    return {
        "inverse_tiles": noise(seeds[0], (NB, BW, NB, BW), 1.0, 6.0, ((0, 8), (2, 32))),
        "factor_panels": noise(seeds[1], (SN, NB, BW, BW), (NA * BW) ** -0.5, 0.0390625, ((1, 32), (2, 8))),
        "ancestors": draw_ancestors(jax.random.fold_in(seeds[5], 71), 0),
        "valid_flags": draw_valid_flags(jax.random.fold_in(seeds[5], 71), 0),
        "block_slot": jax.random.permutation(seeds[4], NB).astype(jnp.int32),
    }


def membership(ancestors, valid_flags, block_slot):
    blocks = jnp.arange(NB, dtype=jnp.int32)
    pick = (ancestors[:, :, None] == blocks[None, None, :]).astype(jnp.int32)
    slots = jnp.sum(pick * block_slot[None, None, :], axis=2)
    hits = (slots[:, :, None] == blocks[None, None, :]) & (valid_flags[:, :, None] == 1)
    return jnp.any(hits, axis=1)


def reference(inverse_tiles, factor_panels, ancestors, valid_flags, block_slot):
    member = membership(ancestors, valid_flags, block_slot)
    masked = jnp.where(member[:, :, None, None], factor_panels, jnp.zeros((), factor_panels.dtype))
    group_len = (NB // N_ROW) * BW
    right = jnp.transpose(masked, (1, 2, 0, 3)).reshape(N_ROW, group_len, SN * BW).astype(jnp.float32)
    left = inverse_tiles.reshape(NB, BW, N_ROW, group_len)

    def one_block(rows):
        grouped = jnp.transpose(rows, (1, 0, 2)).astype(jnp.float32)
        parts = jnp.einsum("grk,gkc->grc", grouped, right)
        return jnp.sum(parts, axis=0)

    product = lax.map(one_block, left).reshape(NB, BW, SN, BW)
    rowmask = jnp.transpose(member)[:, None, :, None]
    return jnp.where(rowmask, -product, jnp.zeros((), product.dtype))
```

```python
import jax
import jax.numpy as jnp
from jax import lax
from jax.experimental import pallas as pl
from jax.experimental.pallas import tpu as pltpu
from jax.sharding import PartitionSpec as P


NZ = 8
STEPS = 4
TOP = 32000.0
TAIL = 16


def membership(ancestors, valid_flags, block_slot):
    blocks = jnp.arange(block_slot.shape[0], dtype=jnp.int32)
    pick = (ancestors[:, :, None] == blocks[None, None, :]).astype(jnp.int32)
    slots = jnp.sum(pick * block_slot[None, None, :], axis=2)
    hits = (slots[:, :, None] == blocks[None, None, :]) & (valid_flags[:, :, None] == 1)
    return jnp.any(hits, axis=1)


def row_perm(move, cores=(0, 1)):
    pairs = []
    for r in range(32):
        ylo, z, core = r // 16, (r // 2) % NZ, r % 2
        if core in cores:
            y2, z2, c2 = move(ylo, z, core)
            pairs.append((r, ((y2 % 2) * NZ + z2 % NZ) * 2 + c2 % 2))
    return pairs


def col_perm(dx, dy):
    return [(c, ((c // 2 + dx) % 4) * 2 + (c % 2 + dy) % 2) for c in range(8)]


CORE = row_perm(lambda y, z, c: (y, z, 1 - c))
FIRST = row_perm(lambda y, z, c: (y, z - 1, c), cores=(1,))
ARM = row_perm(lambda y, z, c: (y, z + 1 - 2 * c, c))


def encode(v):
    top = jnp.maximum(jnp.max(jnp.abs(v), axis=0, keepdims=True), 1e-30)
    e = jnp.ceil(jnp.log2(top * (1.0 / TOP)))
    q = jnp.round(v * (1.0 / jnp.exp2(e)))
    tail = jnp.broadcast_to(e, (TAIL, v.shape[1]))
    return q.astype(jnp.int32).astype(jnp.int16), tail.astype(jnp.int32).astype(jnp.int16)


def decode(ref, rows):
    e = ref[rows : rows + TAIL, :].astype(jnp.int32).astype(jnp.float32)
    return ref[0:rows, :].astype(jnp.int32).astype(jnp.float32) * jnp.exp2(e[0:1, :])


def vmem(n):
    return [pl.BlockSpec(memory_space=pltpu.VMEM)] * n


def cost(flops, nbytes):
    return pl.CostEstimate(flops=flops, bytes_accessed=nbytes, transcendentals=0)


def matmul_body(a_ref, b_ref, ap_ref, bp_ref, out_ref):
    out_ref[...] = jnp.dot(a_ref[...], b_ref[...], preferred_element_type=jnp.float32) + jnp.dot(
        ap_ref[...], bp_ref[...], preferred_element_type=jnp.float32
    )


def matmul(a, b, ap, bp):
    m, k = a.shape
    n = b.shape[1]
    tile = m // 2
    return pl.pallas_call(
        matmul_body,
        grid=(m // tile,),
        in_specs=[
            pl.BlockSpec((tile, k), lambda i: (i, 0)),
            pl.BlockSpec((k, n), lambda i: (0, 0)),
            pl.BlockSpec((tile, k), lambda i: (i, 0)),
            pl.BlockSpec((k, n), lambda i: (0, 0)),
        ],
        out_specs=pl.BlockSpec((tile, n), lambda i: (i, 0)),
        out_shape=jax.ShapeDtypeStruct((m, n), jnp.float32),
        cost_estimate=cost(4 * m * n * k, 4 * m * k + 4 * k * n + 4 * m * n),
        name="matmul",
    )(a, b, ap, bp)


def code_body(p_ref, out_ref):
    m = p_ref.shape[0]
    q, tail = encode(p_ref[...])
    out_ref[0:m, :] = q
    out_ref[m : m + TAIL, :] = tail


def code(p):
    m, n = p.shape
    return pl.pallas_call(
        code_body,
        in_specs=vmem(1),
        out_specs=vmem(1)[0],
        out_shape=jax.ShapeDtypeStruct((m + TAIL, n), jnp.int16),
        cost_estimate=cost(8 * m * n, 6 * m * n),
        name="code",
    )(p)


def join_body(q_ref, p_ref, out_ref):
    m = p_ref.shape[0]
    q, tail = encode(decode(q_ref, m) + p_ref[...])
    out_ref[0:m, :] = q
    out_ref[m : m + TAIL, :] = tail


def join(q, p):
    m, n = p.shape
    return pl.pallas_call(
        join_body,
        in_specs=vmem(2),
        out_specs=vmem(1)[0],
        out_shape=jax.ShapeDtypeStruct((m + TAIL, n), jnp.int16),
        cost_estimate=cost(8 * m * n, 8 * m * n),
        name="join",
    )(q, p)


def split_body(at_ref, q_ref, p_ref, own_ref, *out_refs):
    m = p_ref.shape[0]
    part = m // 4
    keep = jnp.where(at_ref[1] == 0, 1.0, 0.0)
    e = q_ref[m : m + TAIL, :].astype(jnp.int32).astype(jnp.float32)
    scale = jnp.exp2(e[0:1, :])
    for k in range(4):
        rows = pl.ds(pl.multiple_of((at_ref[0] ^ k) * part, part), part)
        v = q_ref[rows, :].astype(jnp.int32).astype(jnp.float32) * scale + p_ref[rows, :] * keep
        if k == 0:
            own_ref[...] = v
        else:
            q, tail = encode(v)
            out_refs[k - 1][0:part, :] = q
            out_refs[k - 1][part : part + TAIL, :] = tail


def split(at, q, p):
    m, n = p.shape
    part = m // 4
    return pl.pallas_call(
        split_body,
        in_specs=[pl.BlockSpec(memory_space=pltpu.SMEM)] + vmem(2),
        out_specs=vmem(4),
        out_shape=[jax.ShapeDtypeStruct((part, n), jnp.float32)]
        + [jax.ShapeDtypeStruct((part + TAIL, n), jnp.int16)] * 3,
        cost_estimate=cost(8 * m * n, 8 * m * n),
        name="split",
    )(at, q, p)


def close_body(own_ref, a_ref, b_ref, c_ref, out_ref):
    m = own_ref.shape[0]
    out_ref[...] = -(own_ref[...] + decode(a_ref, m) + decode(b_ref, m) + decode(c_ref, m))


def close(own, a, b, c):
    return pl.pallas_call(
        close_body,
        in_specs=vmem(4),
        out_specs=vmem(1)[0],
        out_shape=jax.ShapeDtypeStruct(own.shape, jnp.float32),
        cost_estimate=cost(8 * own.size, 14 * own.size),
        name="close",
    )(own, a, b, c)


def per_device(inverse_tiles, factor_panels, ancestors, valid_flags, block_slot):
    local_rows, width, local_cols, _ = inverse_tiles.shape
    count = factor_panels.shape[0]
    row, col = lax.axis_index("row"), lax.axis_index("col")
    core, z, ylo = row % 2, (row // 2) % NZ, row // (2 * NZ)

    member = membership(ancestors, valid_flags, block_slot)
    col_member = lax.dynamic_slice_in_dim(member, row * local_cols, local_cols, 1)
    row_member = lax.dynamic_slice_in_dim(member, col * local_rows, local_rows, 1)

    own_panels, pair_panels = [], []
    for s in range(count):
        shard = factor_panels[s]
        whole = jnp.zeros((local_cols, 8, width // 8, width), shard.dtype)
        whole = lax.dynamic_update_slice(whole, shard[:, None], (0, col, 0, 0))
        for dx, dy in ((0, 1), (2, 1), (1, 1), (3, 1), (2, 0), (1, 0), (3, 0)):
            got = lax.ppermute(shard, "col", col_perm(dx, dy))
            source = ((col // 2 - dx) % 4) * 2 + (col % 2 - dy) % 2
            whole = lax.dynamic_update_slice(whole, got[:, None], (0, source, 0, 0))
        whole = jnp.where(col_member[s][:, None, None, None], whole, jnp.zeros((), whole.dtype))
        whole = whole.reshape(local_cols * width, width)
        own_panels.append(whole)
        pair_panels.append(lax.ppermute(whole, "row", CORE))

    tiles = inverse_tiles.reshape(local_rows, 2, NZ, 2, width // 32, local_cols, width)

    def chunk(zd):
        t = lax.dynamic_index_in_dim(tiles, zd % NZ, 2, keepdims=False)
        return jnp.transpose(t, (1, 2, 0, 3, 4, 5)).reshape(-1, local_cols * width)

    def dest(c, t):
        up = z if t == 1 else z + 5 - t
        return jnp.where(c == 1, z - 5 + t, up)

    theirs = [lax.ppermute(chunk(dest(1 - core, t) + NZ), "row", CORE) for t in range(1, STEPS + 1)]
    mine = [chunk(dest(core, t) + NZ) for t in range(1, STEPS + 1)]

    at = jnp.stack([ylo * 2 + core, core]).astype(jnp.int32)
    results = []
    for s in range(count):
        parts = [matmul(mine[t], own_panels[s], theirs[t], pair_panels[s]) for t in range(STEPS)]
        moving = lax.ppermute(code(parts[0]), "row", FIRST)
        for t in range(1, STEPS):
            moving = lax.ppermute(join(moving, parts[t]), "row", ARM)
        own, *rest = split(at, moving, parts[0])
        got = [
            lax.ppermute(
                rest[k - 1], "row", row_perm(lambda y, zz, c, k=k: (y ^ (k >> 1), zz, c ^ (k & 1)))
            )
            for k in range(1, 4)
        ]
        results.append(close(own, *got).reshape(local_rows, width // 32, width))
    stacked = jnp.stack(results, axis=2)
    rowmask = jnp.transpose(row_member)[:, None, :, None]
    return jnp.where(rowmask, stacked, jnp.zeros((), jnp.float32))


def solution(mesh):
    return jax.shard_map(
        per_device,
        mesh=mesh,
        in_specs=(P("col", None, "row", None), P(None, "row", "col", None), P(), P(), P()),
        out_specs=P("col", "row", None, None),
        check_vma=False,
    )
```

```python
import math

import jax
import jax.numpy as jnp
from jax import lax
from jax.experimental import pallas as pl
from jax.experimental.pallas import tpu as pltpu
from jax.sharding import PartitionSpec as P


NZ = 8
STEPS = 4
EARLY = 4
TOP = 32000.0
TAIL = 16


def membership(ancestors, valid_flags, block_slot):
    blocks = jnp.arange(block_slot.shape[0], dtype=jnp.int32)
    pick = (ancestors[:, :, None] == blocks[None, None, :]).astype(jnp.int32)
    slots = jnp.sum(pick * block_slot[None, None, :], axis=2)
    hits = (slots[:, :, None] == blocks[None, None, :]) & (valid_flags[:, :, None] == 1)
    return jnp.any(hits, axis=1)


def row_perm(move, cores=(0, 1)):
    pairs = []
    for r in range(32):
        ylo, z, core = r // 16, (r // 2) % NZ, r % 2
        if core in cores:
            y2, z2, c2 = move(ylo, z, core)
            pairs.append((r, ((y2 % 2) * NZ + z2 % NZ) * 2 + c2 % 2))
    return pairs


def col_perm(dx, dy):
    return [(c, ((c // 2 + dx) % 4) * 2 + (c % 2 + dy) % 2) for c in range(8)]


CORE = row_perm(lambda y, z, c: (y, z, 1 - c))
FIRST = row_perm(lambda y, z, c: (y, z - 1, c), cores=(1,))
ARM = row_perm(lambda y, z, c: (y, z + 1 - 2 * c, c))


def encode(v):
    top = jnp.maximum(jnp.max(jnp.abs(v), axis=0, keepdims=True), 1e-30)
    e = jnp.ceil(jnp.log2(top * (1.0 / TOP)))
    q = jnp.round(v * jnp.exp2(-e))
    tail = jnp.broadcast_to(e, (TAIL, v.shape[1]))
    return q.astype(jnp.int32).astype(jnp.int16), tail.astype(jnp.int32).astype(jnp.int16)


def scale_of(ref, rows):
    e = ref[rows : rows + TAIL, :].astype(jnp.int32).astype(jnp.float32)
    return jnp.exp2(e[0:1, :])


def decode(ref, rows):
    return ref[0:rows, :].astype(jnp.int32).astype(jnp.float32) * scale_of(ref, rows)


LARGE = 113 << 19
VMEM = pl.BlockSpec(memory_space=pltpu.VMEM)
SMEM = pl.BlockSpec(memory_space=pltpu.SMEM)
HBM = pl.BlockSpec(memory_space=pltpu.HBM)


def call(body, in_specs, out_shape, flops, nbytes, scratch=(), limit=8 << 20):
    many = isinstance(out_shape, list)
    return pl.pallas_call(
        body,
        in_specs=in_specs,
        out_specs=[VMEM] * len(out_shape) if many else VMEM,
        out_shape=out_shape,
        scratch_shapes=list(scratch),
        compiler_params=pltpu.CompilerParams(vmem_limit_bytes=limit),
        cost_estimate=pl.CostEstimate(flops=flops, bytes_accessed=nbytes, transcendentals=0),
    )


def shape(dims, dtype):
    return pltpu.VMEM(dims, dtype)


def gather_body(at_ref, keep_ref, *refs):
    *pieces, out_ref = refs
    count, cols, _, width = pieces[0].shape
    for p, piece in enumerate(pieces):
        for s in range(count):
            for b in range(cols):
                value = piece[s, b]
                keep = jnp.full(value.shape, keep_ref[s * cols + b], jnp.int32) > 0
                out_ref[b, at_ref[p], :, s * width : (s + 1) * width] = jnp.where(
                    keep, value, jnp.zeros_like(value)
                )


def assemble(at, keep, pieces):
    count, cols, rows, width = pieces[0].shape
    out = shape((cols, len(pieces), rows, count * width), pieces[0].dtype)
    f = call(gather_body, [SMEM, SMEM] + [VMEM] * len(pieces), out, 0, 4 * math.prod(out.shape))
    return f(at, keep, *pieces).reshape(-1, count * width)


def fetch(at, a_ref, buf, sem):
    return [pltpu.make_async_copy(a_ref.at[:, y, at], buf.at[y], sem.at[y]) for y in range(2)]


def flat(x):
    return x.reshape(-1, x.shape[2] * x.shape[3])


def put(out_ref, y, r):
    half = r.shape[0] // 2
    r = r.reshape(-1, 2, 8, r.shape[1])
    for c in range(2):
        start = (2 * y + c) * half
        out_ref[start : start + half, :] = r[:, c].reshape(half, r.shape[3])


def prepare_body(at_ref, a_ref, out_ref, buf, sem):
    for o in range(EARLY):
        for copy in fetch(at_ref[o], a_ref, buf.at[o], sem.at[o]):
            copy.start()
    for o in range(EARLY):
        for y, copy in enumerate(fetch(at_ref[o], a_ref, buf.at[o], sem.at[o])):
            copy.wait()
            out_ref[o, y] = flat(buf[o, y])


def prepare(at, a):
    count, ys, zs, rows, cols, width = a.shape
    f = call(
        prepare_body,
        [SMEM, HBM],
        shape((EARLY, ys, count * rows, cols * width), a.dtype),
        0,
        4 * a.size // zs * EARLY,
        [
            pltpu.VMEM((EARLY, ys, count, rows, cols, width), a.dtype),
            pltpu.SemaphoreType.DMA((EARLY, ys)),
        ],
        limit=LARGE,
    )
    return f(at, a)


def first_body(o, a_ref, b_ref, out_ref):
    for y in range(2):
        put(out_ref, y, jnp.dot(a_ref[o, y], b_ref[...], preferred_element_type=jnp.float32))


def first(o, a, b):
    m, (k, n) = a.shape[1] * a.shape[2], b.shape
    f = call(
        lambda *refs: first_body(o, *refs),
        [VMEM, VMEM],
        shape((m, n), jnp.float32),
        2 * m * n * k,
        2 * m * k + 4 * m * n,
    )
    return f(a, b)


def later_body(o, at_ref, a_ref, b_ref, out_ref, buf, sem):
    for copy in fetch(at_ref[o], a_ref, buf, sem):
        copy.start()
    for y, copy in enumerate(fetch(at_ref[o], a_ref, buf, sem)):
        copy.wait()
        put(out_ref, y, jnp.dot(flat(buf[y]), b_ref[...], preferred_element_type=jnp.float32))


def later(o, at, a, b):
    count, ys, _, rows, cols, width = a.shape
    _, n = b.shape
    m = ys * count * rows
    f = call(
        lambda *refs: later_body(o, *refs),
        [SMEM, HBM, VMEM],
        shape((m, n), jnp.float32),
        m * n,
        m,
        [pltpu.VMEM((ys, count, rows, cols, width), a.dtype), pltpu.SemaphoreType.DMA((ys,))],
        limit=LARGE,
    )
    return f(at, a, b)


def step_body(s, first, *refs):
    *q_ref, own_ref, other_ref, out_ref = refs
    m = own_ref.shape[0]
    n = out_ref.shape[1]
    v = own_ref[:, s * n : (s + 1) * n] + other_ref[:, s * n : (s + 1) * n]
    if not first:
        v = v + decode(q_ref[0], m)
    out_ref[0:m, :], out_ref[m : m + TAIL, :] = encode(v)


def step(s, n, q, own, other):
    m = own.shape[0]
    qs = [] if q is None else [q]
    f = call(
        lambda *refs: step_body(s, q is None, *refs),
        [VMEM] * (len(qs) + 2),
        shape((m + TAIL, n), jnp.int16),
        8 * m * n,
        12 * m * n,
    )
    return f(*qs, own, other)


def split_body(s, at_ref, q_ref, own_ref, other_ref, mine_ref, *out_refs):
    m = own_ref.shape[0]
    n = q_ref.shape[1]
    part = m // 4
    up = jnp.full((1, n), at_ref[1], jnp.int32) == 0
    scale = scale_of(q_ref, m)
    cols = slice(s * n, (s + 1) * n)
    for k in range(4):
        rows = pl.ds(pl.multiple_of((at_ref[0] ^ k) * part, part), part)
        v = q_ref[rows, :].astype(jnp.int32).astype(jnp.float32) * scale
        v = v + jnp.where(up, own_ref[rows, cols] + other_ref[rows, cols], 0.0)
        if k == 0:
            mine_ref[...] = v
        else:
            out_refs[k - 1][0:part, :], out_refs[k - 1][part : part + TAIL, :] = encode(v)


def split(s, at, q, own, other):
    m = own.shape[0]
    n = q.shape[1]
    part = m // 4
    f = call(
        lambda *refs: split_body(s, *refs),
        [SMEM] + [VMEM] * 3,
        [shape((part, n), jnp.float32)] + [shape((part + TAIL, n), jnp.int16)] * 3,
        8 * m * n,
        12 * m * n,
    )
    return f(at, q, own, other)


def close_body(keep_ref, *refs):
    *in_refs, out_ref = refs
    m, count, n = out_ref.shape
    for s in range(count):
        mine, *got = in_refs[4 * s : 4 * s + 4]
        v = mine[...] + sum(decode(g, m) for g in got)
        out_ref[:, s, :] = jnp.where(keep_ref[:, s * n : (s + 1) * n] > 0, -v, 0.0)


def close(keep, streams):
    m, n = streams[0][0].shape
    count = len(streams)
    f = call(
        close_body,
        [VMEM] * (1 + 4 * count),
        jax.ShapeDtypeStruct((m, count, n), jnp.float32),
        8 * count * m * n,
        14 * count * m * n,
    )
    return f(keep, *[x for stream in streams for x in stream])


def per_device(inverse_tiles, factor_panels, ancestors, valid_flags, block_slot):
    local_rows, width, local_cols, _ = inverse_tiles.shape
    count = factor_panels.shape[0]
    row, col = lax.axis_index("row"), lax.axis_index("col")
    core, z, ylo = row % 2, (row // 2) % NZ, row // (2 * NZ)
    x, yhi = col // 2, col % 2

    across = lax.ppermute(factor_panels, "col", col_perm(0, 1))
    direct = [lax.ppermute(factor_panels, "col", col_perm(d, 0)) for d in (2, 1, 3)]
    onward = [lax.ppermute(across, "col", col_perm(d, 0)) for d in (2, 1, 3)]
    places = [col, x * 2 + 1 - yhi]
    places += [((x - d) % 4) * 2 + yhi for d in (2, 1, 3)]
    places += [((x - d) % 4) * 2 + 1 - yhi for d in (2, 1, 3)]

    ancestors, across = lax.optimization_barrier((ancestors, across))
    member = membership(ancestors, valid_flags, block_slot)
    col_member = lax.dynamic_slice_in_dim(member, row * local_cols, local_cols, 1)
    row_member = lax.dynamic_slice_in_dim(member, col * local_rows, local_rows, 1)
    rowmask = jnp.repeat(jnp.transpose(row_member).astype(jnp.float32), width // 32, axis=0)
    rowmask = jnp.repeat(rowmask, width, axis=1)

    tiles = inverse_tiles.reshape(local_rows, 2, NZ, width // 16, local_cols, width)

    panels = assemble(
        jnp.stack(places).astype(jnp.int32),
        col_member.reshape(-1).astype(jnp.int32),
        [factor_panels, across] + direct + onward,
    )

    def dest(c, t):
        up = z if t == 1 else z + 5 - t
        return (jnp.where(c == 1, z - 5 + t, up) + NZ) % NZ

    at = jnp.stack([dest(c, t) for t in range(1, STEPS + 1) for c in (1 - core, core)])
    at = at.astype(jnp.int32)
    early = prepare(at, tiles)

    def terms(t, at):
        def multiply(o):
            n = 2 * (t - 1) + o
            return first(n, early, panels) if n < EARLY else later(n, at, tiles, panels)

        theirs = multiply(0)
        other = lax.ppermute(theirs, "row", CORE)
        return multiply(1), other

    here = jnp.stack([ylo * 2 + core, core]).astype(jnp.int32)
    parts = [terms(t, at) for t in range(1, STEPS + 1)]
    moving = [None] * count
    for t in range(1, STEPS + 1):
        for s in range(count):
            coded = step(s, width, moving[s], *parts[t - 1])
            moving[s] = lax.ppermute(coded, "row", FIRST if t == 1 else ARM)
    streams = []
    for s in range(count):
        mine, *rest = split(s, here, moving[s], *parts[0])
        got = [
            lax.ppermute(
                rest[k - 1], "row", row_perm(lambda y, zz, c, k=k: (y ^ (k >> 1), zz, c ^ (k & 1)))
            )
            for k in range(1, 4)
        ]
        streams.append([mine] + got)
    return close(rowmask, streams).reshape(local_rows, width // 32, count, width)


def solution(mesh):
    return jax.shard_map(
        per_device,
        mesh=mesh,
        in_specs=(P("col", None, "row", None), P(None, "row", "col", None), P(), P(), P()),
        out_specs=P("col", "row", None, None),
        check_vma=False,
    )
```

```python
import math

import jax
import jax.numpy as jnp
from jax import lax
from jax.experimental import pallas as pl
from jax.experimental.pallas import tpu as pltpu
from jax.sharding import PartitionSpec as P


NZ = 8
STEPS = 4
HERE = 8 * STEPS
PLACES = HERE + 2
EARLY = 3
TOP = 32000.0
TAIL = 16


def membership(ancestors, valid_flags, block_slot):
    blocks = jnp.arange(block_slot.shape[0], dtype=jnp.int32)
    pick = (ancestors[:, :, None] == blocks[None, None, :]).astype(jnp.int32)
    slots = jnp.sum(pick * block_slot[None, None, :], axis=2)
    hits = (slots[:, :, None] == blocks[None, None, :]) & (valid_flags[:, :, None] == 1)
    return jnp.any(hits, axis=1)


def row_perm(move, cores=(0, 1)):
    pairs = []
    for r in range(32):
        ylo, z, core = r // 16, (r // 2) % NZ, r % 2
        if core in cores:
            y2, z2, c2 = move(ylo, z, core)
            pairs.append((r, ((y2 % 2) * NZ + z2 % NZ) * 2 + c2 % 2))
    return pairs


def col_perm(dx, dy):
    return [(c, ((c // 2 + dx) % 4) * 2 + (c % 2 + dy) % 2) for c in range(8)]


CORE = row_perm(lambda y, z, c: (y, z, 1 - c))
YLO = row_perm(lambda y, z, c: (1 - y, z, c))
ARM = row_perm(lambda y, z, c: (y, z + 1 - 2 * c, c))
ARM_CROSSED = row_perm(lambda y, z, c: (y, z + 1 - 2 * c, 1 - c))


def exponent(top):
    return jnp.ceil(jnp.log2(jnp.maximum(top, 1e-30) * (1.0 / TOP)))


def quantize(v, e):
    return jnp.round(v * jnp.exp2(-e)).astype(jnp.int32).astype(jnp.int16)


def tail(e):
    return jnp.broadcast_to(e, (TAIL, e.shape[1])).astype(jnp.int32).astype(jnp.int16)


def encode(v):
    e = exponent(jnp.max(jnp.abs(v), axis=0, keepdims=True))
    return quantize(v, e), tail(e)


def scale_of(ref, rows):
    e = ref[rows : rows + TAIL, :].astype(jnp.int32).astype(jnp.float32)
    return jnp.exp2(e[0:1, :])


def decode(ref, rows):
    return ref[0:rows, :].astype(jnp.int32).astype(jnp.float32) * scale_of(ref, rows)


VMEM = pl.BlockSpec(memory_space=pltpu.VMEM)
SMEM = pl.BlockSpec(memory_space=pltpu.SMEM)
HBM = pl.BlockSpec(memory_space=pltpu.HBM)


def call(body, in_specs, out_shape, flops, nbytes, scratch=(), limit=8 << 20):
    many = isinstance(out_shape, list)
    return pl.pallas_call(
        body,
        in_specs=in_specs,
        out_specs=[VMEM] * len(out_shape) if many else VMEM,
        out_shape=out_shape,
        scratch_shapes=list(scratch),
        compiler_params=pltpu.CompilerParams(vmem_limit_bytes=limit),
        cost_estimate=pl.CostEstimate(flops=flops, bytes_accessed=nbytes, transcendentals=0),
    )


def shape(dims, dtype):
    return pltpu.VMEM(dims, dtype)


def gather_body(at_ref, keep_ref, *refs):
    *pieces, out_ref = refs
    count, cols, _, width = pieces[0].shape
    for p, piece in enumerate(pieces):
        for s in range(count):
            for b in range(cols):
                value = piece[s, b]
                keep = jnp.full(value.shape, keep_ref[s * cols + b], jnp.int32) > 0
                out_ref[b, at_ref[PLACES + p], :, s * width : (s + 1) * width] = jnp.where(
                    keep, value, jnp.zeros_like(value)
                )


def assemble(at, keep, pieces):
    count, cols, rows, width = pieces[0].shape
    out = shape((cols, len(pieces), rows, count * width), pieces[0].dtype)
    f = call(gather_body, [SMEM, SMEM] + [VMEM] * len(pieces), out, 0, 4 * math.prod(out.shape))
    return f(at, keep, *pieces).reshape(-1, count * width)


def fetch(at_ref, o, a_ref, buf, sem):
    return [
        pltpu.make_async_copy(
            a_ref.at[:, at_ref[4 * o + 2 * h + 1], at_ref[4 * o + 2 * h]], buf.at[h], sem.at[h]
        )
        for h in range(2)
    ]


def flat(x):
    return x.reshape(-1, x.shape[2] * x.shape[3])


def put(out_ref, y, r):
    half = r.shape[0] // 2
    r = r.reshape(-1, 2, 8, r.shape[1])
    for c in range(2):
        start = (2 * y + c) * half
        out_ref[start : start + half, :] = r[:, c].reshape(half, r.shape[3])


def prepare_body(offset, at_ref, a_ref, *refs):
    *out_refs, buf, sem = refs
    count = 2 * len(out_refs)
    for o in range(count):
        for copy in fetch(at_ref, offset + o, a_ref, buf.at[o], sem.at[o]):
            copy.start()
    for o in range(count):
        for y, copy in enumerate(fetch(at_ref, offset + o, a_ref, buf.at[o], sem.at[o])):
            copy.wait()
            out_refs[o // 2][o % 2, y] = flat(buf[o, y])


def prepare(offset, steps, at, a, limit):
    count, ys, zs, rows, cols, width = a.shape
    f = call(
        lambda *refs: prepare_body(offset, *refs),
        [SMEM, HBM],
        [shape((2, ys, count * rows, cols * width), a.dtype)] * steps,
        0,
        8 * a.size // zs * steps,
        [
            pltpu.VMEM((2 * steps, ys, count, rows, cols, width), a.dtype),
            pltpu.SemaphoreType.DMA((2 * steps, ys)),
        ],
        limit=limit,
    )
    return f(at, a)


def multiply_body(o, a_ref, b_ref, out_ref):
    for y in range(2):
        put(out_ref, y, jnp.dot(a_ref[o, y], b_ref[...], preferred_element_type=jnp.float32))


def multiply(o, a, b):
    m, (k, n) = a.shape[1] * a.shape[2], b.shape
    f = call(
        lambda *refs: multiply_body(o, *refs),
        [VMEM, VMEM],
        shape((m, n), jnp.float32),
        2 * m * n * k,
        2 * m * k + 4 * m * n,
    )
    return f(a, b)


def decoded(q_ref, rows, scale):
    return q_ref[rows, :].astype(jnp.int32).astype(jnp.float32) * scale


def code_body(s, own_ref, other_ref, out_ref):
    half, n = own_ref.shape[0] // 2, out_ref.shape[1]
    cols = slice(s * n, (s + 1) * n)
    v = own_ref[0:half, cols] + other_ref[0:half, cols]
    out_ref[0:half, :], out_ref[half : half + TAIL, :] = encode(v)


def code(s, n, own, other):
    half = own.shape[0] // 2
    out = shape((half + TAIL, n), jnp.int16)
    f = call(lambda *r: code_body(s, *r), [VMEM] * 2, out, 4 * half * n, 12 * half * n)
    return f(own, other)


def meet_body(s, at_ref, q_ref, own_ref, other_ref, out_ref):
    m, n = own_ref.shape[0], out_ref.shape[1]
    half = m // 2
    cols = slice(s * n, (s + 1) * n)
    near = pl.ds(pl.multiple_of(at_ref[HERE + 1] * half, half), half)
    far = pl.ds(pl.multiple_of((1 - at_ref[HERE + 1]) * half, half), half)
    v = own_ref[near, cols] + other_ref[near, cols] + decode(q_ref, half)
    w = own_ref[far, cols] + other_ref[far, cols]
    top = jnp.maximum(jnp.abs(v), jnp.abs(w))
    e = exponent(jnp.max(top, axis=0, keepdims=True))
    out_ref[near, :] = quantize(v, e)
    out_ref[far, :] = quantize(w, e)
    out_ref[m : m + TAIL, :] = tail(e)


def meet(s, at, q, own, other):
    m, n = own.shape[0], q.shape[1]
    out = shape((m + TAIL, n), jnp.int16)
    f = call(lambda *r: meet_body(s, *r), [SMEM] + [VMEM] * 3, out, 8 * m * n, 12 * m * n)
    return f(at, q, own, other)


def join_body(s, q_ref, own_ref, other_ref, out_ref):
    m, n = own_ref.shape[0], out_ref.shape[1]
    cols = slice(s * n, (s + 1) * n)
    v = own_ref[:, cols] + other_ref[:, cols] + decode(q_ref, m)
    out_ref[0:m, :], out_ref[m : m + TAIL, :] = encode(v)


def join(s, q, own, other):
    m, n = own.shape[0], q.shape[1]
    out = shape((m + TAIL, n), jnp.int16)
    f = call(lambda *r: join_body(s, *r), [VMEM] * 3, out, 8 * m * n, 12 * m * n)
    return f(q, own, other)


def last_body(s, at_ref, q_ref, own_ref, other_ref, *out_refs):
    m, n = own_ref.shape[0], q_ref.shape[1]
    part = m // 4
    scale = scale_of(q_ref, m)
    cols = slice(s * n, (s + 1) * n)
    for k, out in enumerate(out_refs):
        vs = []
        for y in range(2):
            start = pl.multiple_of((2 * y + (at_ref[HERE + 1] ^ k)) * part, part)
            rows = pl.ds(start, part)
            vs.append(own_ref[rows, cols] + other_ref[rows, cols] + decoded(q_ref, rows, scale))
        top = jnp.maximum(jnp.abs(vs[0]), jnp.abs(vs[1]))
        e = exponent(jnp.max(top, axis=0, keepdims=True))
        for y in range(2):
            out[y * part : (y + 1) * part, :] = quantize(vs[y], e)
        out[2 * part : 2 * part + TAIL, :] = tail(e)


def last(s, at, q, own, other):
    m, n = own.shape[0], q.shape[1]
    outs = [shape((m // 2 + TAIL, n), jnp.int16)] * 2
    f = call(lambda *r: last_body(s, *r), [SMEM] + [VMEM] * 3, outs, 8 * m * n, 12 * m * n)
    return f(at, q, own, other)


def share_body(at_ref, own_ref, other_ref, mine_ref, out_ref):
    part = mine_ref.shape[0]
    for k, ref in enumerate((mine_ref, out_ref)):
        start = pl.multiple_of((2 + (at_ref[HERE + 1] ^ k)) * part, part)
        ref[...] = own_ref[pl.ds(start, part), :] + other_ref[pl.ds(start, part), :]


def share(at, own, other):
    m, n = own.shape
    outs = [shape((m // 4, n), jnp.float32)] * 2
    f = call(share_body, [SMEM] + [VMEM] * 2, outs, m * n, 12 * m * n)
    return f(at, own, other)


def fold_body(s, at_ref, a_ref, b_ref, mine_ref, other_ref, keep_ref, out_ref):
    part, n = keep_ref.shape
    cols = slice(s * n, (s + 1) * n)
    ylo, core = at_ref[HERE], at_ref[HERE + 1]
    scales = [scale_of(r, 2 * part) for r in (a_ref, b_ref)]
    for k in range(2):
        y = ylo ^ k
        rows = pl.ds(pl.multiple_of(y * part, part), part)
        from_mine = jnp.full((part, n), y ^ core, jnp.int32) == 0
        v = jnp.where(from_mine, mine_ref[:, cols], other_ref[:, cols])
        for r, scale in zip((a_ref, b_ref), scales):
            v = v + decoded(r, rows, scale)
        if k == 0:
            keep_ref[...] = v
        else:
            out_ref[0:part, :], out_ref[part : part + TAIL, :] = encode(v)


def fold(s, at, a, b, mine, other):
    part, n = mine.shape[0], a.shape[1]
    outs = [shape((part, n), jnp.float32), shape((part + TAIL, n), jnp.int16)]
    f = call(lambda *r: fold_body(s, *r), [SMEM] + [VMEM] * 4, outs, 8 * part * n, 12 * part * n)
    return f(at, a, b, mine, other)


def close_body(rows, keep_ref, *refs):
    *in_refs, out_ref = refs
    m, count, _ = out_ref.shape
    for s in range(count):
        v = -(in_refs[2 * s][...] + decode(in_refs[2 * s + 1], m))
        for i in range(m // rows):
            block = v[i * rows : (i + 1) * rows]
            keep = jnp.full(block.shape, keep_ref[i * count + s], jnp.int32) > 0
            out_ref[i * rows : (i + 1) * rows, s, :] = jnp.where(keep, block, 0.0)


def close(keep, rows, streams):
    m, n = streams[0][0].shape
    count = len(streams)
    f = call(
        lambda *r: close_body(rows, *r),
        [SMEM] + [VMEM] * (2 * count),
        jax.ShapeDtypeStruct((m, count, n), jnp.float32),
        8 * count * m * n,
        14 * count * m * n,
    )
    return f(keep, *[x for stream in streams for x in stream])


def per_device(inverse_tiles, factor_panels, ancestors, valid_flags, block_slot):
    local_rows, width, local_cols, _ = inverse_tiles.shape
    count = factor_panels.shape[0]
    row, col = lax.axis_index("row"), lax.axis_index("col")
    core, z, ylo = row % 2, (row // 2) % NZ, row // (2 * NZ)
    x, yhi = col // 2, col % 2

    across = lax.ppermute(factor_panels, "col", col_perm(0, 1))
    direct = [lax.ppermute(factor_panels, "col", col_perm(d, 0)) for d in (2, 1, 3)]
    onward = [lax.ppermute(across, "col", col_perm(d, 0)) for d in (2, 1, 3)]
    member = membership(ancestors, valid_flags, block_slot)
    col_member = lax.dynamic_slice_in_dim(member, row * local_cols, local_cols, 1)
    row_member = lax.dynamic_slice_in_dim(member, col * local_rows, local_rows, 1)
    col_keep = col_member.reshape(-1).astype(jnp.int32)
    row_keep = jnp.transpose(row_member).reshape(-1).astype(jnp.int32)

    at = []
    for t in range(1, STEPS + 1):
        for c in (1 - core, core):
            if t == 1:
                at += [(z + NZ // 2) % NZ, c, z, c]
            else:
                zd = (z + NZ + (1 - 2 * c) * (5 - t)) % NZ
                at += [zd, 0, zd, 1]
    at += [ylo, core, col, x * 2 + 1 - yhi]
    at += [((x - d) % 4) * 2 + yhi for d in (2, 1, 3)]
    at += [((x - d) % 4) * 2 + 1 - yhi for d in (2, 1, 3)]
    at = jnp.stack([jnp.asarray(v, jnp.int32) for v in at])

    panels = assemble(at, col_keep, [factor_panels, across] + direct + onward)

    tiles = inverse_tiles.reshape(local_rows, 2, NZ, width // 16, local_cols, width)
    ready = list(prepare(0, EARLY, at, tiles, 54 << 20))
    ready += prepare(2 * EARLY, STEPS - EARLY, at, tiles, 50 << 20)

    def terms(t):
        theirs = multiply(0, ready[t - 1], panels)
        other = lax.ppermute(theirs, "row", CORE)
        return multiply(1, ready[t - 1], panels), other

    parts = [terms(t) for t in range(1, STEPS + 1)]
    mine, rest = share(at, *parts[0])
    shared = lax.ppermute(rest, "row", CORE)
    moving = [None] * count
    for t in range(1, STEPS):
        for s in range(count):
            if t == 1:
                coded = code(s, width, *parts[0])
            elif t == 2:
                coded = meet(s, at, moving[s], *parts[1])
            else:
                coded = join(s, moving[s], *parts[t - 1])
            moving[s] = lax.ppermute(coded, "row", ARM)
    streams = []
    for s in range(count):
        straight, crossed = last(s, at, moving[s], *parts[STEPS - 1])
        crossed = lax.ppermute(crossed, "row", ARM_CROSSED)
        straight = lax.ppermute(straight, "row", ARM)
        kept, sent = fold(s, at, straight, crossed, mine, shared)
        streams.append([kept, lax.ppermute(sent, "row", YLO)])
    out = close(row_keep, width // 32, streams)
    return out.reshape(local_rows, width // 32, count, width)


def solution(mesh):
    return jax.shard_map(
        per_device,
        mesh=mesh,
        in_specs=(P("col", None, "row", None), P(None, "row", "col", None), P(), P(), P()),
        out_specs=P("col", "row", None, None),
        check_vma=False,
    )
```

```python
import math

import jax
import jax.numpy as jnp
from jax import lax
from jax.experimental import pallas as pl
from jax.experimental.pallas import tpu as pltpu
from jax.sharding import PartitionSpec as P


NZ = 8
STEPS = 4
TOP = 32000.0
TAIL = 16


def row_perm(move, cores=(0, 1)):
    pairs = []
    for r in range(32):
        ylo, z, core = r // 16, (r // 2) % NZ, r % 2
        if core in cores:
            y2, z2, c2 = move(ylo, z, core)
            pairs.append((r, ((y2 % 2) * NZ + z2 % NZ) * 2 + c2 % 2))
    return pairs


def place():
    row = lax.axis_index("row")
    return row // (2 * NZ), (row // 2) % NZ, row % 2


def col_perm(dx, dy):
    return [(c, ((c // 2 + dx) % 4) * 2 + (c % 2 + dy) % 2) for c in range(8)]


MOVES = ((0, 0), (0, 1), (2, 0), (1, 0), (3, 0), (2, 1), (1, 1), (3, 1))
CORE = row_perm(lambda y, z, c: (y, z, 1 - c))
YLO = row_perm(lambda y, z, c: (1 - y, z, c))
ARM = row_perm(lambda y, z, c: (y, z + 1 - 2 * c, c))
ARM_CROSSED = row_perm(lambda y, z, c: (y, z + 1 - 2 * c, 1 - c))


def exponent(top):
    return jnp.ceil(jnp.log2(jnp.maximum(top, 1e-30) * (1.0 / TOP)))


def quantize(v, e):
    return jnp.round(v * jnp.exp2(-e)).astype(jnp.int32).astype(jnp.int16)


def tail(e):
    return jnp.broadcast_to(e, (TAIL, e.shape[1])).astype(jnp.int32).astype(jnp.int16)


def encode(v):
    e = exponent(jnp.max(jnp.abs(v), axis=0, keepdims=True))
    return quantize(v, e), tail(e)


def scale_of(ref, rows):
    e = ref[rows : rows + TAIL, :].astype(jnp.int32).astype(jnp.float32)
    return jnp.exp2(e[0:1, :])


def decode(ref, rows):
    return ref[0:rows, :].astype(jnp.int32).astype(jnp.float32) * scale_of(ref, rows)


def decoded(q_ref, rows, scale):
    return q_ref[rows, :].astype(jnp.int32).astype(jnp.float32) * scale


VMEM = pl.BlockSpec(memory_space=pltpu.VMEM)
HBM = pl.BlockSpec(memory_space=pltpu.HBM)


def call(body, in_specs, out_shape, flops, nbytes, scratch=(), limit=8 << 20):
    many = isinstance(out_shape, list)
    return pl.pallas_call(
        body,
        in_specs=in_specs,
        out_specs=[VMEM] * len(out_shape) if many else VMEM,
        out_shape=out_shape,
        scratch_shapes=list(scratch),
        compiler_params=pltpu.CompilerParams(vmem_limit_bytes=limit),
        cost_estimate=pl.CostEstimate(flops=flops, bytes_accessed=nbytes, transcendentals=0),
    )


def shape(dims, dtype):
    return pltpu.VMEM(dims, dtype)


def members_body(ancestors_ref, flags_ref, slot_ref, out_ref):
    n = slot_ref.shape[1]
    count, entries = ancestors_ref.shape
    block = lax.broadcasted_iota(jnp.int32, (n, n), 0)
    slots = (jnp.broadcast_to(slot_ref[...], (n, n)) == block).astype(jnp.float32)
    for s in range(count):
        ids = jnp.broadcast_to(ancestors_ref[s : s + 1, :], (n, entries))
        used = jnp.broadcast_to(flags_ref[s : s + 1, :], (n, entries)) == 1
        named = (ids == block[:, 0:entries]) & used
        hits = jnp.dot(
            slots.astype(jnp.bfloat16),
            named.astype(jnp.float32).astype(jnp.bfloat16),
            preferred_element_type=jnp.float32,
        )
        member = jnp.max(hits, axis=1, keepdims=True)
        out_ref[s] = jnp.broadcast_to(member, out_ref.shape[1:])


def members(ancestors, flags, slot, width):
    count, n = ancestors.shape[0], slot.shape[0]
    out = shape((count, n, width), jnp.float32)
    f = call(members_body, [VMEM] * 3, out, 4 * n * n * n, 4 * n * n)
    return f(ancestors, flags, slot.reshape(1, n))


def gather_body(keep_ref, *refs):
    *pieces, out_ref = refs
    count, cols, rows, width = pieces[0].shape
    col = lax.axis_index("col")
    x, yhi = col // 2, col % 2
    for p, piece in enumerate(pieces):
        dx, dy = MOVES[p]
        at = ((x + 4 - dx) % 4) * 2 + (yhi + dy) % 2
        for s in range(count):
            for b in range(cols):
                block = lax.axis_index("row") * cols + b
                keep = jnp.broadcast_to(keep_ref[s, pl.ds(block, 1), :], (rows, width)) > 0
                value = piece[s, b].astype(jnp.float32)
                value = jnp.where(keep, value, 0.0).astype(piece.dtype)
                out_ref[b, at, :, s * width : (s + 1) * width] = value


def assemble(keep, pieces):
    count, cols, rows, width = pieces[0].shape
    out = shape((cols, len(pieces), rows, count * width), pieces[0].dtype)
    f = call(gather_body, [VMEM] * (1 + len(pieces)), out, 0, 4 * math.prod(out.shape))
    return f(keep, *pieces).reshape(-1, count * width)


def source(o):
    _, z, core = place()
    if o == 0:
        far = (z + NZ // 2) % NZ
        return (far, 1 - core), (far, core)
    c = core if o % 2 else 1 - core
    zd = z if o == 1 else (z + NZ + (1 - 2 * c) * (STEPS - o // 2)) % NZ
    return (zd, 0), (zd, 1)


def fetch(o, a_ref, buf, sem):
    return [
        pltpu.make_async_copy(a_ref.at[:, y, z], buf.at[h], sem.at[h])
        for h, (z, y) in enumerate(source(o))
    ]


def flat(x):
    return x.reshape(-1, x.shape[2] * x.shape[3])


def put(out_ref, y, r):
    half = r.shape[0] // 2
    r = r.reshape(-1, 2, 8, r.shape[1])
    for c in range(2):
        start = (2 * y + c) * half
        out_ref[start : start + half, :] = r[:, c].reshape(half, r.shape[3])


def prepare_body(a_ref, *refs):
    *out_refs, buf, sem = refs
    for o in range(len(out_refs)):
        for copy in fetch(o, a_ref, buf.at[o], sem.at[o]):
            copy.start()
    for o, out_ref in enumerate(out_refs):
        for h, copy in enumerate(fetch(o, a_ref, buf.at[o], sem.at[o])):
            copy.wait()
            out_ref[h] = flat(buf[o, h])


def prepare(a):
    count, ys, _, rows, cols, width = a.shape
    outs = 2 * STEPS
    f = call(
        prepare_body,
        [HBM],
        [shape((ys, count * rows, cols * width), a.dtype)] * outs,
        0,
        4 * a.size,
        [pltpu.VMEM((outs, ys, count, rows, cols, width), a.dtype), pltpu.SemaphoreType.DMA((outs, ys))],
        limit=48 << 20,
    )
    return f(a)


def multiply_body(halves, a_ref, b_ref, out_ref):
    for i, h in enumerate(halves):
        put(out_ref, i, jnp.dot(a_ref[h], b_ref[...], preferred_element_type=jnp.float32))


def multiply(halves, a, b):
    m, (k, n) = a.shape[1] * len(halves), b.shape
    f = call(
        lambda *refs: multiply_body(halves, *refs),
        [VMEM, VMEM],
        shape((m, n), jnp.float32),
        2 * m * n * k,
        2 * m * k + 4 * m * n,
    )
    return f(a, b)


def code_body(s, own_ref, other_ref, out_ref):
    half, n = own_ref.shape[0], out_ref.shape[1]
    cols = slice(s * n, (s + 1) * n)
    v = own_ref[:, cols] + other_ref[:, cols]
    out_ref[0:half, :], out_ref[half : half + TAIL, :] = encode(v)


def code(s, n, own, other):
    half = own.shape[0]
    out = shape((half + TAIL, n), jnp.int16)
    f = call(lambda *r: code_body(s, *r), [VMEM] * 2, out, 4 * half * n, 12 * half * n)
    return f(own, other)


def meet_body(s, q_ref, own_ref, other_ref, out_ref):
    m, n = own_ref.shape[0], out_ref.shape[1]
    half = m // 2
    core = place()[2]
    cols = slice(s * n, (s + 1) * n)
    near = pl.ds(pl.multiple_of(core * half, half), half)
    far = pl.ds(pl.multiple_of((1 - core) * half, half), half)
    v = own_ref[near, cols] + other_ref[near, cols] + decode(q_ref, half)
    w = own_ref[far, cols] + other_ref[far, cols]
    top = jnp.maximum(jnp.abs(v), jnp.abs(w))
    e = exponent(jnp.max(top, axis=0, keepdims=True))
    out_ref[near, :] = quantize(v, e)
    out_ref[far, :] = quantize(w, e)
    out_ref[m : m + TAIL, :] = tail(e)


def meet(s, q, own, other):
    m, n = own.shape[0], q.shape[1]
    out = shape((m + TAIL, n), jnp.int16)
    f = call(lambda *r: meet_body(s, *r), [VMEM] * 3, out, 8 * m * n, 12 * m * n)
    return f(q, own, other)


def join_body(s, q_ref, own_ref, other_ref, out_ref):
    m, n = own_ref.shape[0], out_ref.shape[1]
    cols = slice(s * n, (s + 1) * n)
    v = own_ref[:, cols] + other_ref[:, cols] + decode(q_ref, m)
    out_ref[0:m, :], out_ref[m : m + TAIL, :] = encode(v)


def join(s, q, own, other):
    m, n = own.shape[0], q.shape[1]
    out = shape((m + TAIL, n), jnp.int16)
    f = call(lambda *r: join_body(s, *r), [VMEM] * 3, out, 8 * m * n, 12 * m * n)
    return f(q, own, other)


def last_body(s, q_ref, own_ref, other_ref, *out_refs):
    m, n = own_ref.shape[0], q_ref.shape[1]
    part = m // 4
    core = place()[2]
    scale = scale_of(q_ref, m)
    cols = slice(s * n, (s + 1) * n)
    for k, out in enumerate(out_refs):
        vs = []
        for y in range(2):
            start = pl.multiple_of((2 * y + (core ^ k)) * part, part)
            rows = pl.ds(start, part)
            vs.append(own_ref[rows, cols] + other_ref[rows, cols] + decoded(q_ref, rows, scale))
        top = jnp.maximum(jnp.abs(vs[0]), jnp.abs(vs[1]))
        e = exponent(jnp.max(top, axis=0, keepdims=True))
        for y in range(2):
            out[y * part : (y + 1) * part, :] = quantize(vs[y], e)
        out[2 * part : 2 * part + TAIL, :] = tail(e)


def last(s, q, own, other):
    m, n = own.shape[0], q.shape[1]
    outs = [shape((m // 2 + TAIL, n), jnp.int16)] * 2
    f = call(lambda *r: last_body(s, *r), [VMEM] * 3, outs, 8 * m * n, 12 * m * n)
    return f(q, own, other)


def near_body(a_ref, b_ref, mine_ref, theirs_ref):
    part = mine_ref.shape[0] // 2
    first = jnp.full((part, b_ref.shape[1]), place()[2], jnp.int32) == 0
    for y in range(2):
        r = jnp.dot(a_ref[y], b_ref[...], preferred_element_type=jnp.float32)
        r = r.reshape(-1, 2, 8, r.shape[1])
        r = [r[:, c].reshape(part, r.shape[3]) for c in range(2)]
        rows = slice(y * part, (y + 1) * part)
        mine_ref[rows, :] = jnp.where(first, r[0], r[1])
        theirs_ref[rows, :] = jnp.where(first, r[1], r[0])


def near(a, b):
    m, (k, n) = a.shape[0] * a.shape[1], b.shape
    outs = [shape((m // 2, n), jnp.float32)] * 2
    return call(near_body, [VMEM] * 2, outs, 2 * m * n * k, 2 * m * k + 4 * m * n)(a, b)


def fold_body(s, a_ref, b_ref, mine_ref, other_ref, keep_ref, out_ref):
    part, n = keep_ref.shape
    cols = slice(s * n, (s + 1) * n)
    ylo = place()[0]
    scales = [scale_of(r, 2 * part) for r in (a_ref, b_ref)]
    for k in range(2):
        y = ylo ^ k
        rows = pl.ds(pl.multiple_of(y * part, part), part)
        v = mine_ref[rows, cols] + other_ref[rows, cols]
        for r, scale in zip((a_ref, b_ref), scales):
            v = v + decoded(r, rows, scale)
        if k == 0:
            keep_ref[...] = v
        else:
            out_ref[0:part, :], out_ref[part : part + TAIL, :] = encode(v)


def fold(s, a, b, mine, other):
    part, n = mine.shape[0] // 2, a.shape[1]
    outs = [shape((part, n), jnp.float32), shape((part + TAIL, n), jnp.int16)]
    f = call(lambda *r: fold_body(s, *r), [VMEM] * 4, outs, 8 * part * n, 12 * part * n)
    return f(a, b, mine, other)


def close_body(rows, keep_ref, *refs):
    *in_refs, out_ref = refs
    m, count, _ = out_ref.shape
    for s in range(count):
        v = -(in_refs[2 * s][...] + decode(in_refs[2 * s + 1], m))
        for i in range(m // rows):
            block = v[i * rows : (i + 1) * rows]
            own = lax.axis_index("col") * (m // rows) + i
            keep = jnp.broadcast_to(keep_ref[s, pl.ds(own, 1), :], block.shape) > 0
            out_ref[i * rows : (i + 1) * rows, s, :] = jnp.where(keep, block, 0.0)


def close(keep, rows, streams):
    m, n = streams[0][0].shape
    count = len(streams)
    f = call(
        lambda *r: close_body(rows, *r),
        [VMEM] * (1 + 2 * count),
        jax.ShapeDtypeStruct((m, count, n), jnp.float32),
        8 * count * m * n,
        14 * count * m * n,
    )
    return f(keep, *[x for stream in streams for x in stream])


def per_device(inverse_tiles, factor_panels, ancestors, valid_flags, block_slot):
    local_rows, width, local_cols, _ = inverse_tiles.shape
    count = factor_panels.shape[0]

    across = lax.ppermute(factor_panels, "col", col_perm(0, 1))
    pieces = [factor_panels, across]
    pieces += [lax.ppermute(factor_panels, "col", col_perm(*move)) for move in MOVES[2:5]]
    pieces += [lax.ppermute(across, "col", col_perm(dx, 0)) for dx, _ in MOVES[5:8]]
    keep = members(ancestors, valid_flags, block_slot, width)
    panels = assemble(keep, pieces)

    ready = prepare(inverse_tiles.reshape(local_rows, 2, NZ, width // 16, local_cols, width))

    def terms(t):
        theirs = multiply((0,), ready[0], panels) if t == 1 else multiply((0, 1), ready[2 * t - 2], panels)
        other = lax.ppermute(theirs, "row", CORE)
        mine = multiply((1,), ready[0], panels) if t == 1 else multiply((0, 1), ready[2 * t - 1], panels)
        return mine, other

    parts = [terms(t) for t in range(1, STEPS + 1)]
    mine, rest = near(ready[1], panels)
    shared = lax.ppermute(rest, "row", CORE)
    moving = [None] * count
    streams = []
    for t in range(1, STEPS + 1):
        for s in range(count):
            if t == 1:
                coded = code(s, width, *parts[0])
            elif t == 2:
                coded = meet(s, moving[s], *parts[1])
            elif t < STEPS:
                coded = join(s, moving[s], *parts[t - 1])
            else:
                straight, crossed = last(s, moving[s], *parts[t - 1])
            if t < STEPS:
                moving[s] = lax.ppermute(coded, "row", ARM)
            else:
                crossed = lax.ppermute(crossed, "row", ARM_CROSSED)
                straight = lax.ppermute(straight, "row", ARM)
            if t == STEPS:
                kept, sent = fold(s, straight, crossed, mine, shared)
                streams.append([kept, lax.ppermute(sent, "row", YLO)])
    out = close(keep, width // 32, streams)
    return out.reshape(local_rows, width // 32, count, width)


def solution(mesh):
    return jax.shard_map(
        per_device,
        mesh=mesh,
        in_specs=(P("col", None, "row", None), P(None, "row", "col", None), P(), P(), P()),
        out_specs=P("col", "row", None, None),
        check_vma=False,
    )
```

```python
import math

import jax
import jax.numpy as jnp
from jax import lax
from jax.experimental import pallas as pl
from jax.experimental.pallas import tpu as pltpu
from jax.sharding import PartitionSpec as P


NZ = 8
STEPS = 4
TOP = 32000.0
TAIL = 16


def row_perm(move, cores=(0, 1)):
    pairs = []
    for r in range(32):
        ylo, z, core = r // 16, (r // 2) % NZ, r % 2
        if core in cores:
            y2, z2, c2 = move(ylo, z, core)
            pairs.append((r, ((y2 % 2) * NZ + z2 % NZ) * 2 + c2 % 2))
    return pairs


def place():
    row = lax.axis_index("row")
    return row // (2 * NZ), (row // 2) % NZ, row % 2


def col_perm(dx, dy):
    return [(c, ((c // 2 + dx) % 4) * 2 + (c % 2 + dy) % 2) for c in range(8)]


MOVES = ((0, 0), (0, 1), (2, 0), (1, 0), (3, 0), (2, 1), (1, 1), (3, 1))
CORE = row_perm(lambda y, z, c: (y, z, 1 - c))
YLO = row_perm(lambda y, z, c: (1 - y, z, c))
ARM = row_perm(lambda y, z, c: (y, z + 1 - 2 * c, c))
ARM_CROSSED = row_perm(lambda y, z, c: (1 - y, z + 1 - 2 * c, c))


def exponent(top):
    return jnp.ceil(jnp.log2(jnp.maximum(top, 1e-30) * (1.0 / TOP)))


def quantize(v, e):
    return jnp.round(v * jnp.exp2(-e)).astype(jnp.int32).astype(jnp.int16)


def tail(e):
    return jnp.broadcast_to(e, (TAIL, e.shape[1])).astype(jnp.int32).astype(jnp.int16)


def encode(v):
    e = exponent(jnp.max(jnp.abs(v), axis=0, keepdims=True))
    return quantize(v, e), tail(e)


def scale_of(ref, rows):
    e = ref[rows : rows + TAIL, :].astype(jnp.int32).astype(jnp.float32)
    return jnp.exp2(e[0:1, :])


def decode(ref, rows):
    return ref[0:rows, :].astype(jnp.int32).astype(jnp.float32) * scale_of(ref, rows)


def decoded(q_ref, rows, scale):
    return q_ref[rows, :].astype(jnp.int32).astype(jnp.float32) * scale


VMEM = pl.BlockSpec(memory_space=pltpu.VMEM)
HBM = pl.BlockSpec(memory_space=pltpu.HBM)


def call(body, in_specs, out_shape, flops, nbytes, scratch=(), limit=8 << 20):
    many = isinstance(out_shape, list)
    return pl.pallas_call(
        body,
        in_specs=in_specs,
        out_specs=[VMEM] * len(out_shape) if many else VMEM,
        out_shape=out_shape,
        scratch_shapes=list(scratch),
        compiler_params=pltpu.CompilerParams(vmem_limit_bytes=limit),
        cost_estimate=pl.CostEstimate(flops=flops, bytes_accessed=nbytes, transcendentals=0),
    )


def shape(dims, dtype):
    return pltpu.VMEM(dims, dtype)


def members_body(ancestors_ref, flags_ref, slot_ref, out_ref):
    n = slot_ref.shape[1]
    count, entries = ancestors_ref.shape
    block = lax.broadcasted_iota(jnp.int32, (n, n), 0)
    slots = (jnp.broadcast_to(slot_ref[...], (n, n)) == block).astype(jnp.float32)
    for s in range(count):
        ids = jnp.broadcast_to(ancestors_ref[s : s + 1, :], (n, entries))
        used = jnp.broadcast_to(flags_ref[s : s + 1, :], (n, entries)) == 1
        named = (ids == block[:, 0:entries]) & used
        hits = jnp.dot(
            slots.astype(jnp.bfloat16),
            named.astype(jnp.float32).astype(jnp.bfloat16),
            preferred_element_type=jnp.float32,
        )
        member = jnp.max(hits, axis=1, keepdims=True)
        out_ref[s] = jnp.broadcast_to(member, out_ref.shape[1:])


def members(ancestors, flags, slot, width):
    count, n = ancestors.shape[0], slot.shape[0]
    out = shape((count, n, width), jnp.float32)
    f = call(members_body, [VMEM] * 3, out, 4 * n * n * n, 4 * n * n)
    return f(ancestors, flags, slot.reshape(1, n))


def gather_body(keep_ref, *refs):
    *pieces, out_ref = refs
    count, cols, rows, width = pieces[0].shape
    col = lax.axis_index("col")
    x, yhi = col // 2, col % 2
    for p, piece in enumerate(pieces):
        dx, dy = MOVES[p]
        at = ((x + 4 - dx) % 4) * 2 + (yhi + dy) % 2
        for s in range(count):
            for b in range(cols):
                block = lax.axis_index("row") * cols + b
                keep = jnp.broadcast_to(keep_ref[s, pl.ds(block, 1), :], (rows, width)) > 0
                value = piece[s, b].astype(jnp.float32)
                value = jnp.where(keep, value, 0.0).astype(piece.dtype)
                out_ref[b, at, :, s * width : (s + 1) * width] = value


def assemble(keep, pieces):
    count, cols, rows, width = pieces[0].shape
    out = shape((cols, len(pieces), rows, count * width), pieces[0].dtype)
    f = call(gather_body, [VMEM] * (1 + len(pieces)), out, 0, 4 * math.prod(out.shape))
    return f(keep, *pieces).reshape(-1, count * width)


def source(o):
    _, z, core = place()
    if o == 0:
        far = (z + NZ // 2) % NZ
        return (far, 1 - core), (far, core)
    c = core if o % 2 else 1 - core
    zd = z if o == 1 else (z + NZ + (1 - 2 * c) * (STEPS - o // 2)) % NZ
    return (zd, 0), (zd, 1)


def fetch(o, a_ref, buf, sem):
    return [
        pltpu.make_async_copy(a_ref.at[:, y, z], buf.at[h], sem.at[h])
        for h, (z, y) in enumerate(source(o))
    ]


def flat(x):
    return x.reshape(-1, x.shape[2] * x.shape[3])


def put(out_ref, y, r):
    half = r.shape[0] // 2
    r = r.reshape(-1, 2, 8, r.shape[1])
    for c in range(2):
        start = (2 * y + c) * half
        out_ref[start : start + half, :] = r[:, c].reshape(half, r.shape[3])


def prepare_body(a_ref, *refs):
    *out_refs, buf, sem = refs
    for o in range(len(out_refs)):
        for copy in fetch(o, a_ref, buf.at[o], sem.at[o]):
            copy.start()
    for o, out_ref in enumerate(out_refs):
        for h, copy in enumerate(fetch(o, a_ref, buf.at[o], sem.at[o])):
            copy.wait()
            out_ref[h] = flat(buf[o, h])


def prepare(a):
    count, ys, _, rows, cols, width = a.shape
    outs = 2 * STEPS
    f = call(
        prepare_body,
        [HBM],
        [shape((ys, count * rows, cols * width), a.dtype)] * outs,
        0,
        4 * a.size,
        [pltpu.VMEM((outs, ys, count, rows, cols, width), a.dtype), pltpu.SemaphoreType.DMA((outs, ys))],
        limit=48 << 20,
    )
    return f(a)


def multiply_body(halves, a_ref, b_ref, out_ref):
    for i, h in enumerate(halves):
        put(out_ref, i, jnp.dot(a_ref[h], b_ref[...], preferred_element_type=jnp.float32))


def multiply(halves, a, b):
    m, (k, n) = a.shape[1] * len(halves), b.shape
    f = call(
        lambda *refs: multiply_body(halves, *refs),
        [VMEM, VMEM],
        shape((m, n), jnp.float32),
        2 * m * n * k,
        2 * m * k + 4 * m * n,
    )
    return f(a, b)


def code_body(s, own_ref, other_ref, out_ref):
    half, n = own_ref.shape[0], out_ref.shape[1]
    cols = slice(s * n, (s + 1) * n)
    v = own_ref[:, cols] + other_ref[:, cols]
    out_ref[0:half, :], out_ref[half : half + TAIL, :] = encode(v)


def code(s, n, own, other):
    half = own.shape[0]
    out = shape((half + TAIL, n), jnp.int16)
    f = call(lambda *r: code_body(s, *r), [VMEM] * 2, out, 4 * half * n, 12 * half * n)
    return f(own, other)


def meet_body(s, q_ref, own_ref, other_ref, out_ref):
    m, n = own_ref.shape[0], out_ref.shape[1]
    half = m // 2
    core = place()[2]
    cols = slice(s * n, (s + 1) * n)
    near = pl.ds(pl.multiple_of(core * half, half), half)
    far = pl.ds(pl.multiple_of((1 - core) * half, half), half)
    v = own_ref[near, cols] + other_ref[near, cols] + decode(q_ref, half)
    w = own_ref[far, cols] + other_ref[far, cols]
    top = jnp.maximum(jnp.abs(v), jnp.abs(w))
    e = exponent(jnp.max(top, axis=0, keepdims=True))
    out_ref[near, :] = quantize(v, e)
    out_ref[far, :] = quantize(w, e)
    out_ref[m : m + TAIL, :] = tail(e)


def meet(s, q, own, other):
    m, n = own.shape[0], q.shape[1]
    out = shape((m + TAIL, n), jnp.int16)
    f = call(lambda *r: meet_body(s, *r), [VMEM] * 3, out, 8 * m * n, 12 * m * n)
    return f(q, own, other)


def join_body(s, q_ref, own_ref, other_ref, out_ref):
    m, n = own_ref.shape[0], out_ref.shape[1]
    cols = slice(s * n, (s + 1) * n)
    v = own_ref[:, cols] + other_ref[:, cols] + decode(q_ref, m)
    out_ref[0:m, :], out_ref[m : m + TAIL, :] = encode(v)


def join(s, q, own, other):
    m, n = own.shape[0], q.shape[1]
    out = shape((m + TAIL, n), jnp.int16)
    f = call(lambda *r: join_body(s, *r), [VMEM] * 3, out, 8 * m * n, 12 * m * n)
    return f(q, own, other)


def last_body(s, q_ref, own_ref, other_ref, *out_refs):
    m, n = own_ref.shape[0], q_ref.shape[1]
    half = m // 2
    ylo = place()[0]
    scale = scale_of(q_ref, m)
    cols = slice(s * n, (s + 1) * n)
    for k, out in enumerate(out_refs):
        rows = pl.ds(pl.multiple_of((ylo ^ k) * half, half), half)
        v = own_ref[rows, cols] + other_ref[rows, cols] + decoded(q_ref, rows, scale)
        out[0:half, :], out[half : half + TAIL, :] = encode(v)


def last(s, q, own, other):
    m, n = own.shape[0], q.shape[1]
    outs = [shape((m // 2 + TAIL, n), jnp.int16)] * 2
    f = call(lambda *r: last_body(s, *r), [VMEM] * 3, outs, 8 * m * n, 12 * m * n)
    return f(q, own, other)


def near_body(a_ref, b_ref, mine_ref, theirs_ref):
    half = mine_ref.shape[0]
    ylo = place()[0]
    put(mine_ref, 0, jnp.dot(a_ref[ylo], b_ref[...], preferred_element_type=jnp.float32))
    r = jnp.dot(a_ref[1 - ylo], b_ref[...], preferred_element_type=jnp.float32)
    r = r.reshape(-1, 2, 8, r.shape[1])
    v = jnp.concatenate([r[:, c].reshape(half // 2, r.shape[3]) for c in range(2)], axis=0)
    theirs_ref[0:half, :], theirs_ref[half : half + TAIL, :] = encode(v)


def near(a, b):
    m, (k, n) = a.shape[0] * a.shape[1], b.shape
    outs = [shape((m // 2, n), jnp.float32), shape((m // 2 + TAIL, n), jnp.int16)]
    return call(near_body, [VMEM] * 2, outs, 2 * m * n * k, 2 * m * k + 4 * m * n)(a, b)


def fold_body(s, a_ref, b_ref, mine_ref, other_ref, keep_ref, out_ref):
    part, n = keep_ref.shape
    cols = slice(s * n, (s + 1) * n)
    core = place()[2]
    scales = [scale_of(r, 2 * part) for r in (a_ref, b_ref, other_ref)]
    scales[2] = scales[2][:, cols]
    for k, out in enumerate((keep_ref, out_ref)):
        rows = pl.ds(pl.multiple_of((core ^ k) * part, part), part)
        v = mine_ref[rows, cols] + other_ref[rows, cols].astype(jnp.int32).astype(jnp.float32) * scales[2]
        for r, scale in zip((a_ref, b_ref), scales):
            v = v + decoded(r, rows, scale)
        out[...] = v


def fold(s, a, b, mine, other):
    part, n = mine.shape[0] // 2, a.shape[1]
    outs = [shape((part, n), jnp.float32)] * 2
    f = call(lambda *r: fold_body(s, *r), [VMEM] * 4, outs, 8 * part * n, 12 * part * n)
    return f(a, b, mine, other)


def close_body(rows, keep_ref, *refs):
    *in_refs, out_ref = refs
    m, count, _ = out_ref.shape
    for s in range(count):
        v = -(in_refs[2 * s][...] + in_refs[2 * s + 1][...])
        for i in range(m // rows):
            block = v[i * rows : (i + 1) * rows]
            own = lax.axis_index("col") * (m // rows) + i
            keep = jnp.broadcast_to(keep_ref[s, pl.ds(own, 1), :], block.shape) > 0
            out_ref[i * rows : (i + 1) * rows, s, :] = jnp.where(keep, block, 0.0)


def close(keep, rows, streams):
    m, n = streams[0][0].shape
    count = len(streams)
    f = call(
        lambda *r: close_body(rows, *r),
        [VMEM] * (1 + 2 * count),
        jax.ShapeDtypeStruct((m, count, n), jnp.float32),
        8 * count * m * n,
        14 * count * m * n,
    )
    return f(keep, *[x for stream in streams for x in stream])


def per_device(inverse_tiles, factor_panels, ancestors, valid_flags, block_slot):
    local_rows, width, local_cols, _ = inverse_tiles.shape
    count = factor_panels.shape[0]

    across = lax.ppermute(factor_panels, "col", col_perm(0, 1))
    pieces = [factor_panels, across]
    pieces += [lax.ppermute(factor_panels, "col", col_perm(*move)) for move in MOVES[2:5]]
    pieces += [lax.ppermute(across, "col", col_perm(dx, 0)) for dx, _ in MOVES[5:8]]
    keep = members(ancestors, valid_flags, block_slot, width)
    panels = assemble(keep, pieces)

    ready = prepare(inverse_tiles.reshape(local_rows, 2, NZ, width // 16, local_cols, width))

    def terms(t):
        theirs = multiply((0,), ready[0], panels) if t == 1 else multiply((0, 1), ready[2 * t - 2], panels)
        other = lax.ppermute(theirs, "row", CORE)
        mine = multiply((1,), ready[0], panels) if t == 1 else multiply((0, 1), ready[2 * t - 1], panels)
        return mine, other

    parts = [terms(t) for t in range(1, STEPS + 1)]
    mine, rest = near(ready[1], panels)
    shared = lax.ppermute(rest, "row", YLO)
    moving = [None] * count
    streams = []
    for t in range(1, STEPS + 1):
        for s in range(count):
            if t == 1:
                coded = code(s, width, *parts[0])
            elif t == 2:
                coded = meet(s, moving[s], *parts[1])
            elif t < STEPS:
                coded = join(s, moving[s], *parts[t - 1])
            else:
                straight, crossed = last(s, moving[s], *parts[t - 1])
            if t < STEPS:
                moving[s] = lax.ppermute(coded, "row", ARM)
            else:
                crossed = lax.ppermute(crossed, "row", ARM_CROSSED)
                straight = lax.ppermute(straight, "row", ARM)
            if t == STEPS:
                kept, sent = fold(s, straight, crossed, mine, shared)
                streams.append([kept, lax.ppermute(sent, "row", CORE)])
    out = close(keep, width // 32, streams)
    return out.reshape(local_rows, width // 32, count, width)


def solution(mesh):
    return jax.shard_map(
        per_device,
        mesh=mesh,
        in_specs=(P("col", None, "row", None), P(None, "row", "col", None), P(), P(), P()),
        out_specs=P("col", "row", None, None),
        check_vma=False,
    )
```

```python
import math

import jax
import jax.numpy as jnp
from jax import lax
from jax.experimental import pallas as pl
from jax.experimental.pallas import tpu as pltpu
from jax.sharding import PartitionSpec as P


NZ = 8
STEPS = 4
TOP = 32000.0
TAIL = 16


def row_perm(move, cores=(0, 1)):
    pairs = []
    for r in range(32):
        ylo, z, core = r // 16, (r // 2) % NZ, r % 2
        if core in cores:
            y2, z2, c2 = move(ylo, z, core)
            pairs.append((r, ((y2 % 2) * NZ + z2 % NZ) * 2 + c2 % 2))
    return pairs


def place():
    row = lax.axis_index("row")
    return row // (2 * NZ), (row // 2) % NZ, row % 2


def col_perm(dx, dy):
    return [(c, ((c // 2 + dx) % 4) * 2 + (c % 2 + dy) % 2) for c in range(8)]


MOVES = ((0, 0), (0, 1), (2, 0), (1, 0), (3, 0), (2, 1), (1, 1), (3, 1))
CORE = row_perm(lambda y, z, c: (y, z, 1 - c))
YLO = row_perm(lambda y, z, c: (1 - y, z, c))
ARM = row_perm(lambda y, z, c: (y, z + 1 - 2 * c, c))
ARM_CROSSED = row_perm(lambda y, z, c: (1 - y, z + 1 - 2 * c, c))


def exponent(top):
    return jnp.ceil(jnp.log2(jnp.maximum(top, 1e-30) * (1.0 / TOP)))


def quantize(v, e):
    return jnp.round(v * jnp.exp2(-e)).astype(jnp.int32).astype(jnp.int16)


def tail(e):
    return jnp.broadcast_to(e, (TAIL, e.shape[1])).astype(jnp.int32).astype(jnp.int16)


def encode(v):
    e = exponent(jnp.max(jnp.abs(v), axis=0, keepdims=True))
    return quantize(v, e), tail(e)


def scale_of(ref, rows):
    e = ref[rows : rows + TAIL, :].astype(jnp.int32).astype(jnp.float32)
    return jnp.exp2(e[0:1, :])


def decode(ref, rows):
    return ref[0:rows, :].astype(jnp.int32).astype(jnp.float32) * scale_of(ref, rows)


def decoded(q_ref, rows, scale):
    return q_ref[rows, :].astype(jnp.int32).astype(jnp.float32) * scale


VMEM = pl.BlockSpec(memory_space=pltpu.VMEM)
HBM = pl.BlockSpec(memory_space=pltpu.HBM)


def call(body, in_specs, out_shape, flops, nbytes, scratch=(), limit=8 << 20):
    many = isinstance(out_shape, list)
    return pl.pallas_call(
        body,
        in_specs=in_specs,
        out_specs=[VMEM] * len(out_shape) if many else VMEM,
        out_shape=out_shape,
        scratch_shapes=list(scratch),
        compiler_params=pltpu.CompilerParams(vmem_limit_bytes=limit),
        cost_estimate=pl.CostEstimate(flops=flops, bytes_accessed=nbytes, transcendentals=0),
    )


def shape(dims, dtype):
    return pltpu.VMEM(dims, dtype)


def members_body(ancestors_ref, flags_ref, slot_ref, out_ref):
    n = slot_ref.shape[1]
    count, entries = ancestors_ref.shape
    block = lax.broadcasted_iota(jnp.int32, (n, n), 0)
    slots = (jnp.broadcast_to(slot_ref[...], (n, n)) == block).astype(jnp.float32)
    for s in range(count):
        ids = jnp.broadcast_to(ancestors_ref[s : s + 1, :], (n, entries))
        used = jnp.broadcast_to(flags_ref[s : s + 1, :], (n, entries)) == 1
        named = (ids == block[:, 0:entries]) & used
        hits = jnp.dot(
            slots.astype(jnp.bfloat16),
            named.astype(jnp.float32).astype(jnp.bfloat16),
            preferred_element_type=jnp.float32,
        )
        member = jnp.max(hits, axis=1, keepdims=True)
        out_ref[s] = jnp.broadcast_to(member, out_ref.shape[1:])


def members(ancestors, flags, slot, width):
    count, n = ancestors.shape[0], slot.shape[0]
    out = shape((count, n, width), jnp.float32)
    f = call(members_body, [VMEM] * 3, out, 4 * n * n * n, 4 * n * n)
    return f(ancestors, flags, slot.reshape(1, n))


def gather_body(keep_ref, *refs):
    *pieces, out_ref = refs
    count, cols, rows, width = pieces[0].shape
    col = lax.axis_index("col")
    x, yhi = col // 2, col % 2
    for p, piece in enumerate(pieces):
        dx, dy = MOVES[p]
        at = ((x + 4 - dx) % 4) * 2 + (yhi + dy) % 2
        for s in range(count):
            for b in range(cols):
                block = lax.axis_index("row") * cols + b
                keep = jnp.broadcast_to(keep_ref[s, pl.ds(block, 1), :], (rows, width)) > 0
                value = piece[s, b].astype(jnp.float32)
                value = jnp.where(keep, value, 0.0).astype(piece.dtype)
                out_ref[b, at, :, s * width : (s + 1) * width] = value


def assemble(keep, pieces):
    count, cols, rows, width = pieces[0].shape
    out = shape((cols, len(pieces), rows, count * width), pieces[0].dtype)
    f = call(gather_body, [VMEM] * (1 + len(pieces)), out, 0, 4 * math.prod(out.shape))
    return f(keep, *pieces).reshape(-1, count * width)


def source(o):
    _, z, core = place()
    if o == 0:
        far = (z + NZ // 2) % NZ
        return (far, 1 - core), (far, core)
    c = core if o % 2 else 1 - core
    zd = z if o == 1 else (z + NZ + (1 - 2 * c) * (STEPS - o // 2)) % NZ
    return (zd, 0), (zd, 1)


def fetch(o, a_ref, buf, sem):
    return [
        pltpu.make_async_copy(a_ref.at[:, y, z], buf.at[h], sem.at[h])
        for h, (z, y) in enumerate(source(o))
    ]


def flat(x):
    return x.reshape(-1, x.shape[2] * x.shape[3])


def put(out_ref, y, r):
    half = r.shape[0] // 2
    r = r.reshape(-1, 2, 8, r.shape[1])
    for c in range(2):
        start = (2 * y + c) * half
        out_ref[start : start + half, :] = r[:, c].reshape(half, r.shape[3])


def prepare_body(a_ref, *refs):
    *out_refs, buf, sem = refs
    for o in range(len(out_refs)):
        for copy in fetch(o, a_ref, buf.at[o], sem.at[o]):
            copy.start()
    for o, out_ref in enumerate(out_refs):
        for h, copy in enumerate(fetch(o, a_ref, buf.at[o], sem.at[o])):
            copy.wait()
            out_ref[h] = flat(buf[o, h])


def prepare(a):
    count, ys, _, rows, cols, width = a.shape
    outs = 2 * STEPS
    f = call(
        prepare_body,
        [HBM],
        [shape((ys, count * rows, cols * width), a.dtype)] * outs,
        0,
        4 * a.size,
        [pltpu.VMEM((outs, ys, count, rows, cols, width), a.dtype), pltpu.SemaphoreType.DMA((outs, ys))],
        limit=48 << 20,
    )
    return f(a)


def multiply_body(halves, a_ref, b_ref, out_ref):
    for i, h in enumerate(halves):
        put(out_ref, i, jnp.dot(a_ref[h], b_ref[...], preferred_element_type=jnp.float32))


def multiply(halves, a, b):
    m, (k, n) = a.shape[1] * len(halves), b.shape
    f = call(
        lambda *refs: multiply_body(halves, *refs),
        [VMEM, VMEM],
        shape((m, n), jnp.float32),
        2 * m * n * k,
        2 * m * k + 4 * m * n,
    )
    return f(a, b)


def code_body(s, own_ref, other_ref, out_ref):
    half, n = own_ref.shape[0], out_ref.shape[1]
    cols = slice(s * n, (s + 1) * n)
    v = own_ref[:, cols] + other_ref[:, cols]
    out_ref[0:half, :], out_ref[half : half + TAIL, :] = encode(v)


def code(s, n, own, other):
    half = own.shape[0]
    out = shape((half + TAIL, n), jnp.int16)
    f = call(lambda *r: code_body(s, *r), [VMEM] * 2, out, 4 * half * n, 12 * half * n)
    return f(own, other)


def meet_body(s, q_ref, own_ref, other_ref, out_ref):
    m, n = own_ref.shape[0], out_ref.shape[1]
    half = m // 2
    core = place()[2]
    cols = slice(s * n, (s + 1) * n)
    near = pl.ds(pl.multiple_of(core * half, half), half)
    far = pl.ds(pl.multiple_of((1 - core) * half, half), half)
    v = own_ref[near, cols] + other_ref[near, cols] + decode(q_ref, half)
    w = own_ref[far, cols] + other_ref[far, cols]
    top = jnp.maximum(jnp.abs(v), jnp.abs(w))
    e = exponent(jnp.max(top, axis=0, keepdims=True))
    out_ref[near, :] = quantize(v, e)
    out_ref[far, :] = quantize(w, e)
    out_ref[m : m + TAIL, :] = tail(e)


def meet(s, q, own, other):
    m, n = own.shape[0], q.shape[1]
    out = shape((m + TAIL, n), jnp.int16)
    f = call(lambda *r: meet_body(s, *r), [VMEM] * 3, out, 8 * m * n, 12 * m * n)
    return f(q, own, other)


def join_body(s, q_ref, own_ref, other_ref, out_ref):
    m, n = own_ref.shape[0], out_ref.shape[1]
    cols = slice(s * n, (s + 1) * n)
    v = own_ref[:, cols] + other_ref[:, cols] + decode(q_ref, m)
    out_ref[0:m, :], out_ref[m : m + TAIL, :] = encode(v)


def join(s, q, own, other):
    m, n = own.shape[0], q.shape[1]
    out = shape((m + TAIL, n), jnp.int16)
    f = call(lambda *r: join_body(s, *r), [VMEM] * 3, out, 8 * m * n, 12 * m * n)
    return f(q, own, other)


def last_body(s, q_ref, own_ref, other_ref, *out_refs):
    m, n = own_ref.shape[0], q_ref.shape[1]
    half = m // 2
    ylo = place()[0]
    scale = scale_of(q_ref, m)
    cols = slice(s * n, (s + 1) * n)
    for k, out in enumerate(out_refs):
        rows = pl.ds(pl.multiple_of((ylo ^ k) * half, half), half)
        v = own_ref[rows, cols] + other_ref[rows, cols] + decoded(q_ref, rows, scale)
        out[0:half, :], out[half : half + TAIL, :] = encode(v)


def last(s, q, own, other):
    m, n = own.shape[0], q.shape[1]
    outs = [shape((m // 2 + TAIL, n), jnp.int16)] * 2
    f = call(lambda *r: last_body(s, *r), [VMEM] * 3, outs, 8 * m * n, 12 * m * n)
    return f(q, own, other)


def near_body(a_ref, b_ref, mine_ref, theirs_ref):
    half = mine_ref.shape[0]
    ylo = place()[0]
    put(mine_ref, 0, jnp.dot(a_ref[ylo], b_ref[...], preferred_element_type=jnp.float32))
    r = jnp.dot(a_ref[1 - ylo], b_ref[...], preferred_element_type=jnp.float32)
    r = r.reshape(-1, 2, 8, r.shape[1])
    v = jnp.concatenate([r[:, c].reshape(half // 2, r.shape[3]) for c in range(2)], axis=0)
    theirs_ref[0:half, :], theirs_ref[half : half + TAIL, :] = encode(v)


def near(a, b):
    m, (k, n) = a.shape[0] * a.shape[1], b.shape
    outs = [shape((m // 2, n), jnp.float32), shape((m // 2 + TAIL, n), jnp.int16)]
    return call(near_body, [VMEM] * 2, outs, 2 * m * n * k, 2 * m * k + 4 * m * n)(a, b)


def fold_body(s, a_ref, b_ref, mine_ref, other_ref, keep_ref, out_ref):
    part, n = keep_ref.shape
    cols = slice(s * n, (s + 1) * n)
    core = place()[2]
    scales = [scale_of(r, 2 * part) for r in (a_ref, b_ref, other_ref)]
    scales[2] = scales[2][:, cols]
    for k, out in enumerate((keep_ref, out_ref)):
        rows = pl.ds(pl.multiple_of((core ^ k) * part, part), part)
        v = mine_ref[rows, cols] + other_ref[rows, cols].astype(jnp.int32).astype(jnp.float32) * scales[2]
        for r, scale in zip((a_ref, b_ref), scales):
            v = v + decoded(r, rows, scale)
        out[...] = v


def fold(s, a, b, mine, other):
    part, n = mine.shape[0] // 2, a.shape[1]
    outs = [shape((part, n), jnp.float32)] * 2
    f = call(lambda *r: fold_body(s, *r), [VMEM] * 4, outs, 8 * part * n, 12 * part * n)
    return f(a, b, mine, other)


def close_body(rows, keep_ref, *refs):
    *in_refs, out_ref = refs
    m, count, _ = out_ref.shape
    for s in range(count):
        v = -(in_refs[2 * s][...] + in_refs[2 * s + 1][...])
        for i in range(m // rows):
            block = v[i * rows : (i + 1) * rows]
            own = lax.axis_index("col") * (m // rows) + i
            keep = jnp.broadcast_to(keep_ref[s, pl.ds(own, 1), :], block.shape) > 0
            out_ref[i * rows : (i + 1) * rows, s, :] = jnp.where(keep, block, 0.0)


def close(keep, rows, streams):
    m, n = streams[0][0].shape
    count = len(streams)
    f = call(
        lambda *r: close_body(rows, *r),
        [VMEM] * (1 + 2 * count),
        jax.ShapeDtypeStruct((m, count, n), jnp.float32),
        8 * count * m * n,
        14 * count * m * n,
    )
    return f(keep, *[x for stream in streams for x in stream])


def per_device(inverse_tiles, factor_panels, ancestors, valid_flags, block_slot):
    local_rows, width, local_cols, _ = inverse_tiles.shape
    count = factor_panels.shape[0]

    across = lax.ppermute(factor_panels, "col", col_perm(0, 1))
    one, three = [lax.ppermute(factor_panels, "col", col_perm(dx, 0)) for dx in (1, 3)]
    onward = []
    for dx, _ in MOVES[5:8]:
        onward.append(lax.ppermute(across, "col", col_perm(dx, 0)))
    two = lax.ppermute(three, "col", col_perm(3, 0))
    pieces = [factor_panels, across, two, one, three] + onward
    keep = members(ancestors, valid_flags, block_slot, width)
    panels = assemble(keep, pieces)

    ready = prepare(inverse_tiles.reshape(local_rows, 2, NZ, width // 16, local_cols, width))

    def terms(t):
        theirs = multiply((0,), ready[0], panels) if t == 1 else multiply((0, 1), ready[2 * t - 2], panels)
        other = lax.ppermute(theirs, "row", CORE)
        mine = multiply((1,), ready[0], panels) if t == 1 else multiply((0, 1), ready[2 * t - 1], panels)
        return mine, other

    parts = [terms(t) for t in range(1, STEPS + 1)]
    mine, rest = near(ready[1], panels)
    shared = lax.ppermute(rest, "row", YLO)
    moving = [None] * count
    streams = []
    for t in range(1, STEPS + 1):
        for s in range(count):
            if t == 1:
                coded = code(s, width, *parts[0])
            elif t == 2:
                coded = meet(s, moving[s], *parts[1])
            elif t < STEPS:
                coded = join(s, moving[s], *parts[t - 1])
            else:
                straight, crossed = last(s, moving[s], *parts[t - 1])
            if t < STEPS:
                moving[s] = lax.ppermute(coded, "row", ARM)
            else:
                crossed = lax.ppermute(crossed, "row", ARM_CROSSED)
                straight = lax.ppermute(straight, "row", ARM)
            if t == STEPS:
                kept, sent = fold(s, straight, crossed, mine, shared)
                streams.append([kept, lax.ppermute(sent, "row", CORE)])
    out = close(keep, width // 32, streams)
    return out.reshape(local_rows, width // 32, count, width)


def solution(mesh):
    return jax.shard_map(
        per_device,
        mesh=mesh,
        in_specs=(P("col", None, "row", None), P(None, "row", "col", None), P(), P(), P()),
        out_specs=P("col", "row", None, None),
        check_vma=False,
    )
```
